256 devices in a mesh: dp: 16 (over z, core), frame: 16 (over y, x).
Axes of the slice: x: 4, y: 4, z: 8, core: 2. Of those that a mesh axis runs over, the one named last changes fastest.
Arguments:
- latents: bfloat16 [16, 16, 512, 640], P('dp', 'frame'), may hold values from -6 to 6
- cotangent: bfloat16 [16, 16, 512, 640], P('dp', 'frame'), may hold values from -6 to 6
- timesteps: int32 [16], P('dp'), may hold values from 0 to 999
- spatial_weight: bfloat16 [9, 640, 640], replicated, may hold values from -0.078125 to 0.078125
- temporal_weight: bfloat16 [3, 640, 640], replicated, may hold values from -0.125 to 0.125
Outputs:
- new_spatial: float32 [9, 640, 640], P(None, 'frame')
- new_temporal: float32 [3, 640, 640], P(None, 'frame')
The draws below stay inside these ranges and needn't reach their ends.
All inputs are finite; a program needn't handle non-finite values.
Results may differ from the reference program's by a relative error of at most 0.02.
Values may be sent and summed in bfloat16 or wider, within the bound.
No kernel may reach another device: no remote copies, remote signals or barrier semaphores. Data moves between devices by JAX's collectives and lax.ppermute only.
A program may use at most 128 MiB of HBM per device.

```python
import math
import jax
import jax.numpy as jnp
from jax import lax

CHANNELS = 640
WIDTH = 64
SLAB = 8
TSTEPS = 1000
PIXELS = 512
FRAMES = 16
SAMPLES = 16


def with_ends(array, stream_key, least, top_value):
    dims = array.shape
    spot = [jax.random.randint(jax.random.fold_in(stream_key, axis), (), 0, dims[axis]) for axis in range(len(dims))]
    array = array.at[tuple(spot)].set(least)
    longest = dims.index(max(dims))
    spot[longest] = (spot[longest] + 1) % dims[longest]
    return array.at[tuple(spot)].set(top_value)


def levels(own_key, dims, shards, low, top_value):
    gain = 1.0
    for position, parts in shards:
        draws = jax.random.uniform(jax.random.fold_in(jax.random.fold_in(own_key, 6), position), (parts,), jnp.float32, low / len(shards), top_value / len(shards))
        gain = gain * jnp.repeat(jnp.exp(draws), dims[position] // parts).reshape((-1,) + (1,) * (len(dims) - 1 - position))
    return gain


def gaussian(rng, extent, deviation, limit, cuts=(), kind=jnp.bfloat16):
    values = jax.random.normal(rng, extent, jnp.float32) * deviation
    if len(cuts) > 0:
        values = levels(rng, extent, cuts, -0.22, 0.18) * values
    return jnp.clip(values, min=-limit, max=limit).astype(kind)


def setup_inputs(seed: int = 0) -> dict:
    splits = jax.random.split(jax.random.key(seed), 6)
    latents = gaussian(splits[0], (SAMPLES, FRAMES, PIXELS, CHANNELS), 1.0, 6.0, ((0, 16), (1, 16)))
    cotangent = gaussian(splits[1], (SAMPLES, FRAMES, PIXELS, CHANNELS), 1.0, 6.0, ((0, 16), (1, 16)))
    timesteps = with_ends(jax.random.randint(splits[2], (SAMPLES,), 0, TSTEPS), jax.random.fold_in(splits[2], 1), 0, TSTEPS - 1).astype(jnp.int32)
    spatial_weight = gaussian(splits[3], (9, CHANNELS, CHANNELS), (9 * CHANNELS) ** -0.5, 0.078125)
    temporal_weight = gaussian(splits[4], (3, CHANNELS, CHANNELS), (3 * CHANNELS) ** -0.5, 0.125)
    return dict(latents=latents, cotangent=cotangent, timesteps=timesteps, spatial_weight=spatial_weight, temporal_weight=temporal_weight)


def embed(timesteps, channels):
    half_width = channels // 2
    frequencies = jnp.exp(-math.log(10000.0) * jnp.arange(half_width, dtype=jnp.float32) / half_width)
    angles = timesteps.astype(jnp.float32)[:, None] * frequencies[None, :]
    return jnp.concatenate([jnp.sin(angles), jnp.cos(angles)], axis=1)

def unfold(activated, slab_rows, grid_width):
    lead_count, pixels, channels = activated.shape
    grid_cells = activated.reshape(lead_count, slab_rows, grid_width, channels)
    padded = jnp.pad(grid_cells, ((0, 0), (1, 1), (1, 1), (0, 0)))
    pieces = [padded[:, row_off:row_off + slab_rows, col_off:col_off + grid_width, :] for row_off in range(3) for col_off in range(3)]
    return jnp.concatenate(pieces, axis=3).reshape(lead_count, pixels, 9 * channels)

def silu_slope(pre_act):
    logistic = jax.nn.sigmoid(pre_act)
    return logistic * (1.0 + pre_act * (1.0 - logistic))

def clip_factor(squares, channels):
    max_norm = 0.5 * math.sqrt(12.0) * channels
    return jnp.minimum(1.0, max_norm / (jnp.sqrt(squares) + 1e-06))

def reference(latents, cotangent, timesteps, spatial_weight, temporal_weight):
    ws_flat = spatial_weight.reshape(9 * CHANNELS, CHANNELS).astype(jnp.float32)
    wt_full = temporal_weight.astype(jnp.float32)
    shifts = embed(timesteps, CHANNELS)

    def one_sample(totals, inputs):
        sample_x, sample_cot, shift_row = inputs
        activated = jax.nn.silu(sample_x.astype(jnp.float32) + shift_row[None, None, :]).astype(jnp.bfloat16)
        columns = unfold(activated, SLAB, WIDTH).astype(jnp.float32)
        pre_act = jnp.einsum('fpk,kc->fpc', columns, ws_flat)
        gated = jax.nn.silu(pre_act).astype(jnp.bfloat16)
        pad_spec = ((1, 1), (0, 0), (0, 0))
        gated_pad = jnp.pad(gated, pad_spec).astype(jnp.float32)
        cot_pad = jnp.pad(sample_cot, pad_spec).astype(jnp.float32)
        cot_full = sample_cot.astype(jnp.float32)
        temporal_grad = jnp.stack([jnp.einsum('fpc,fpd->cd', gated_pad[offset:offset + FRAMES], cot_full) for offset in range(3)])
        grad_gated = jnp.zeros(pre_act.shape, jnp.float32)
        for offset in range(3):
            grad_gated = grad_gated + jnp.einsum('fpd,cd->fpc', cot_pad[2 - offset:2 - offset + FRAMES], wt_full[offset])
        grad_gated = grad_gated.astype(jnp.bfloat16)
        grad_pre = (grad_gated.astype(jnp.float32) * silu_slope(pre_act)).astype(jnp.bfloat16)
        frame_terms = jnp.einsum('fpk,fpc->fkc', columns, grad_pre.astype(jnp.float32)).astype(jnp.bfloat16)
        frame_terms = lax.optimization_barrier(frame_terms).astype(jnp.float32)
        return ((totals[0] + lax.optimization_barrier(jnp.sum(frame_terms, axis=0)), totals[1] + temporal_grad), None)
    start_totals = (jnp.zeros((9 * CHANNELS, CHANNELS), jnp.float32), jnp.zeros((3, CHANNELS, CHANNELS), jnp.float32))
    grads, unused_out = lax.scan(one_sample, start_totals, (latents, cotangent, shifts))
    spatial_grad = grads[0].reshape(9, CHANNELS, CHANNELS)
    temporal_grad = grads[1]
    squares = jnp.sum(spatial_grad * spatial_grad) + jnp.sum(temporal_grad * temporal_grad)
    factor = clip_factor(squares, CHANNELS)
    return (spatial_weight.astype(jnp.float32) - factor * spatial_grad, temporal_weight.astype(jnp.float32) - factor * temporal_grad)
```

```python
import math

import jax
import jax.numpy as jnp
from jax import lax
from jax.sharding import Mesh
from jax.sharding import PartitionSpec as P


WIDTH = 64
SLAB = 8
F32 = jnp.float32
BF16 = jnp.bfloat16
SIZES = {"z": 8, "core": 2, "y": 4, "x": 4}


def embed(timesteps, channels):
    half_width = channels // 2
    frequencies = jnp.exp(
        -math.log(10000.0) * jnp.arange(half_width, dtype=jnp.float32) / half_width
    )
    angles = timesteps.astype(jnp.float32)[:, None] * frequencies[None, :]
    return jnp.concatenate([jnp.sin(angles), jnp.cos(angles)], axis=1)


def clip_factor(squares, channels):
    max_norm = 0.5 * math.sqrt(12.0) * channels
    return jnp.minimum(1.0, max_norm / (jnp.sqrt(squares) + 1e-06))


def hop(value, axis, step):
    size = SIZES[axis]
    return lax.ppermute(value, axis, [(i, (i + step) % size) for i in range(size)])


def ring_scatter(buf, axis):
    half = buf.shape[1] // 2
    from_left = hop(buf[2, :half], axis, 1)
    from_right = hop(buf[2, half:], axis, 3)
    ahead = jnp.concatenate(
        [(buf[1, :half].astype(F32) + from_left.astype(F32)).astype(BF16), buf[1, half:]], 0
    )
    behind = jnp.concatenate(
        [buf[3, :half], (buf[3, half:].astype(F32) + from_right.astype(F32)).astype(BF16)], 0
    )
    from_left = hop(ahead, axis, 1)
    from_right = hop(behind, axis, 3)
    return (buf[0].astype(F32) + from_left.astype(F32) + from_right.astype(F32)).astype(BF16)


def direct_scatter(buf, axis):
    far = hop(buf[2], axis, 2)
    left = hop(buf[1], axis, 1)
    right = hop(buf[3], axis, 3)
    total = buf[0].astype(F32) + left.astype(F32) + right.astype(F32) + far.astype(F32)
    return total.astype(BF16)


def channel_order(first, second, channels):
    block = channels // 16
    col = lax.broadcasted_iota(jnp.int32, (channels, channels), 1)
    row = lax.broadcasted_iota(jnp.int32, (channels, channels), 0)
    places = {first: col // (4 * block), second: (col // block) % 4}
    y_owner = (lax.axis_index("y") + places["y"]) % 4
    x_owner = (lax.axis_index("x") + places["x"]) % 4
    return (row == (y_owner * 4 + x_owner) * block + col % block).astype(BF16)


def shift_rows(value, by):
    rows = value.shape[1]
    if by == 0:
        return value
    if by > 0:
        return jnp.pad(value[:, by:], ((0, 0), (0, by), (0, 0)))
    return jnp.pad(value[:, : rows + by], ((0, 0), (-by, 0), (0, 0)))


def shift_cols(value, by):
    if by == 0:
        return value
    q = lax.broadcasted_iota(jnp.int32, (1, value.shape[1], 1), 1) % WIDTH
    edge = q == (WIDTH - 1 if by > 0 else 0)
    return jnp.where(edge, jnp.zeros((), value.dtype), shift_rows(value, by))


def dot_rows(left, right):
    return lax.dot_general(left, right, (((0, 1), (0, 1)), ((), ())), preferred_element_type=F32)


def on_device(latents, cotangent, timesteps, spatial_weight, temporal_weight):
    channels = latents.shape[3]
    pixels = latents.shape[2]
    core = lax.axis_index("core")
    first_core = core == 0
    cot = cotangent.reshape(pixels, channels)
    frames = SIZES["y"] * SIZES["x"]
    cot_prev = lax.ppermute(cot, ("y", "x"), [(f, f + 1) for f in range(frames - 1)])
    cot_next = lax.ppermute(cot, ("y", "x"), [(f + 1, f) for f in range(frames - 1)])

    shifts = embed(timesteps, channels)
    activated = jax.nn.silu(latents.reshape(pixels, channels).astype(F32) + shifts).astype(BF16)

    order_a = channel_order("x", "y", channels)
    order_b = channel_order("y", "x", channels)

    def reorder(value, order):
        return jnp.dot(value, order, preferred_element_type=F32).astype(BF16)

    act_a = reorder(activated, order_a)
    act_b = reorder(activated, order_b)
    both = [(0, 1), (1, 0)]
    up = [(0, 1)]
    act_a = jnp.stack([act_a, lax.ppermute(act_a, "core", both)])
    act_b = jnp.stack([act_b, lax.ppermute(act_b, "core", both)])

    pre_act = lax.conv_general_dilated(
        activated.reshape(1, SLAB, WIDTH, channels),
        spatial_weight.reshape(3, 3, channels, channels),
        (1, 1),
        ((1, 1), (1, 1)),
        dimension_numbers=("NHWC", "HWIO", "NHWC"),
        preferred_element_type=F32,
    ).reshape(pixels, channels)
    logistic = jax.nn.sigmoid(pre_act)
    gated = (pre_act * logistic).astype(BF16)
    slope = logistic * (1.0 + pre_act * (1.0 - logistic))
    gated_b = reorder(gated, order_b)
    gated_b = jnp.stack([gated_b, lax.ppermute(gated_b, "core", up)])
    cots = [jnp.stack([c, lax.ppermute(c, "core", up)]) for c in (cot_next, cot, cot_prev)]

    def back(value, k):
        return lax.dot_general(
            value, temporal_weight[k], (((1,), (1,)), ((), ())), preferred_element_type=F32
        )

    grad_gated = (back(cot, 1) + back(cot_next, 0) + back(cot_prev, 2)).astype(BF16)
    grad_pre = (grad_gated.astype(F32) * slope).astype(BF16)
    grad_pre = jnp.stack([grad_pre, lax.ppermute(grad_pre, "core", both)])

    edge_rows = jnp.where(first_core, shift_rows(act_a, -WIDTH), shift_rows(act_a, WIDTH))
    taps_a = [dot_rows(shift_cols(edge_rows, e - 1), grad_pre).astype(BF16) for e in range(3)]
    taps_b = [
        dot_rows(
            jnp.where(first_core, shift_cols(act_b, e - 1), gated_b),
            jnp.where(first_core, grad_pre, cots[e]),
        ).astype(BF16)
        for e in range(3)
    ]
    block = channels // 16

    def shares(taps):
        stacked = jnp.stack([t.reshape(4, 4, block, channels) for t in taps], axis=2)
        return stacked.reshape(4, 12 * block, channels)

    part_a = ring_scatter(shares(taps_a), "x")
    part_b = ring_scatter(shares(taps_b), "y")
    part_a = direct_scatter(part_a.reshape(4, 3 * block, channels), "y")
    part_b = direct_scatter(part_b.reshape(4, 3 * block, channels), "x")
    part = jnp.concatenate([part_a, part_b], 0).reshape(8, 6 * block // 8, channels)
    part = lax.all_to_all(part, "z", 0, 0)
    part = jnp.sum(part.astype(F32), axis=0).astype(BF16)
    part = lax.all_to_all(jnp.broadcast_to(part[None], (8,) + part.shape), "z", 0, 0)
    mine = part.reshape(6, block, channels)
    other = lax.ppermute(mine, "core", both)
    low = jnp.where(first_core, mine, other).astype(F32)
    high = jnp.where(first_core, other, mine).astype(F32)

    squares = (jnp.sum(low * low) + jnp.sum(high * high)).reshape(1, 1) + jnp.zeros((8, 128), F32)
    for axis in ("x", "y"):
        squares = squares + hop(squares, axis, 1) + hop(squares, axis, 2) + hop(squares, axis, 3)
    factor = clip_factor(squares[0, 0], channels)
    row_start = (lax.axis_index("y") * 4 + lax.axis_index("x")) * block
    spatial_here = lax.dynamic_slice(spatial_weight, (0, row_start, 0), (9, block, channels))
    temporal_here = lax.dynamic_slice(temporal_weight, (0, row_start, 0), (3, block, channels))
    spatial_part = jnp.concatenate([low, high[:3]], 0)
    new_spatial = spatial_here.astype(F32) - factor * spatial_part
    new_temporal = temporal_here.astype(F32) - factor * high[3:]
    return (new_spatial, new_temporal)


def solution(mesh):
    names = tuple(SIZES)
    grid = Mesh(mesh.devices.reshape(tuple(SIZES.values())), names)
    rows, frame = ("z", "core"), ("y", "x")
    in_specs = (P(rows, frame, None, None), P(rows, frame, None, None), P(rows), P(), P())
    out_specs = (P(None, frame, None), P(None, frame, None))
    return jax.shard_map(
        on_device, mesh=grid, in_specs=in_specs, out_specs=out_specs, check_vma=False
    )
```

```python
import math

import jax
import jax.numpy as jnp
from jax import lax
from jax.sharding import Mesh
from jax.sharding import PartitionSpec as P


WIDTH = 64
SLAB = 8
F32 = jnp.float32
BF16 = jnp.bfloat16
SIZES = {"z": 8, "core": 2, "y": 4, "x": 4}


def embed(timesteps, channels):
    half_width = channels // 2
    frequencies = jnp.exp(
        -math.log(10000.0) * jnp.arange(half_width, dtype=jnp.float32) / half_width
    )
    angles = timesteps.astype(jnp.float32)[:, None] * frequencies[None, :]
    return jnp.concatenate([jnp.sin(angles), jnp.cos(angles)], axis=1)


def clip_factor(squares, channels):
    max_norm = 0.5 * math.sqrt(12.0) * channels
    return jnp.minimum(1.0, max_norm / (jnp.sqrt(squares) + 1e-06))


def hop(value, axis, step):
    size = SIZES[axis]
    return lax.ppermute(value, axis, [(i, (i + step) % size) for i in range(size)])


def add(left, right):
    return (left.astype(F32) + right.astype(F32)).astype(BF16)


def ahead_of(value, axis, places, dim=0):
    index = (lax.axis_index(axis) + places) % SIZES[axis]
    return lax.dynamic_index_in_dim(value, index, dim, keepdims=False)


def ring_open(share, axis):
    far = share(2)
    half = far.shape[0] // 2
    return hop(far[:half], axis, 1), hop(far[half:], axis, 3)


def ring_close(share, axis, from_left, from_right):
    half = from_left.shape[0]
    ahead = share(1)
    behind = share(3)
    ahead = jnp.concatenate([add(ahead[:half], from_left), ahead[half:]], 0)
    behind = jnp.concatenate([behind[:half], add(behind[half:], from_right)], 0)
    from_left = hop(ahead, axis, 1)
    from_right = hop(behind, axis, 3)
    return (share(0).astype(F32) + from_left.astype(F32) + from_right.astype(F32)).astype(BF16)


def direct_scatter(share, axis):
    far = hop(share(2), axis, 2)
    left = hop(share(1), axis, 1)
    right = hop(share(3), axis, 3)
    total = share(0).astype(F32) + left.astype(F32) + right.astype(F32) + far.astype(F32)
    return total.astype(BF16)


def shift_rows(value, by):
    rows = value.shape[1]
    if by == 0:
        return value
    if by > 0:
        return jnp.pad(value[:, by:], ((0, 0), (0, by), (0, 0)))
    return jnp.pad(value[:, : rows + by], ((0, 0), (-by, 0), (0, 0)))


def shift_cols(value, by):
    if by == 0:
        return value
    q = lax.broadcasted_iota(jnp.int32, (1, value.shape[1], 1), 1) % WIDTH
    edge = q == (WIDTH - 1 if by > 0 else 0)
    return jnp.where(edge, jnp.zeros((), value.dtype), shift_rows(value, by))


def dot_rows(left, right):
    return lax.dot_general(left, right, (((0, 1), (0, 1)), ((), ())), preferred_element_type=F32)


def on_device(latents, cotangent, timesteps, spatial_weight, temporal_weight):
    channels = latents.shape[3]
    pixels = latents.shape[2]
    core = lax.axis_index("core")
    first_core = core == 0
    cot = cotangent.reshape(pixels, channels)
    frames = SIZES["y"] * SIZES["x"]
    frame = lax.axis_index("y") * SIZES["x"] + lax.axis_index("x")
    cot_prev = lax.ppermute(cot, ("y", "x"), [(f, (f + 1) % frames) for f in range(frames)])
    cot_next = lax.ppermute(cot, ("y", "x"), [((f + 1) % frames, f) for f in range(frames)])
    cot_prev = jnp.where(frame == 0, jnp.zeros_like(cot), cot_prev)
    cot_next = jnp.where(frame == frames - 1, jnp.zeros_like(cot), cot_next)

    shifts = embed(timesteps, channels)
    activated = jax.nn.silu(latents.reshape(pixels, channels).astype(F32) + shifts).astype(BF16)

    both = [(0, 1), (1, 0)]
    act = jnp.stack([activated, lax.ppermute(activated, "core", both)])

    pre_act = lax.conv_general_dilated(
        activated.reshape(1, SLAB, WIDTH, channels),
        spatial_weight.reshape(3, 3, channels, channels),
        (1, 1),
        ((1, 1), (1, 1)),
        dimension_numbers=("NHWC", "HWIO", "NHWC"),
        preferred_element_type=F32,
    ).reshape(pixels, channels)
    logistic = jax.nn.sigmoid(pre_act)
    gated = (pre_act * logistic).astype(BF16)
    slope = logistic * (1.0 + pre_act * (1.0 - logistic))
    lent = lax.ppermute(jnp.stack([cot_next, cot, cot_prev, gated]), "core", both)
    cots = [jnp.stack([c, lent[i]]) for i, c in enumerate((cot_next, cot, cot_prev))]
    gates = jnp.stack([gated, lent[3]])

    def back(value, k):
        return lax.dot_general(
            value, temporal_weight[k], (((1,), (1,)), ((), ())), preferred_element_type=F32
        )

    grad_gated = (back(cot, 1) + back(cot_next, 0) + back(cot_prev, 2)).astype(BF16)
    grad_pre = (grad_gated.astype(F32) * slope).astype(BF16)
    grad_pre = jnp.stack([grad_pre, lax.ppermute(grad_pre, "core", both)])

    edge_rows = jnp.where(first_core, shift_rows(act, -WIDTH), shift_rows(act, WIDTH))
    taps_a = [dot_rows(shift_cols(edge_rows, e - 1), grad_pre).astype(BF16) for e in range(3)]
    lefts = [jnp.where(first_core, shift_cols(act, e - 1), gates) for e in range(3)]
    rights = [jnp.where(first_core, grad_pre, cots[e]) for e in range(3)]
    lefts, rights = lax.optimization_barrier((lefts, rights))
    block = channels // 16

    def shares(taps, axis, dim):
        taps = [t.reshape(4, 4, block, channels) for t in taps]

        def share(places):
            picked = [ahead_of(t, axis, places, dim) for t in taps]
            return jnp.stack(picked, axis=1).reshape(12 * block, channels)

        return share

    share_a = shares(taps_a, "x", 1)
    opened = ring_open(share_a, "x")
    taps_b = [dot_rows(l, r).astype(BF16) for l, r in zip(lefts, rights)]
    opened, taps_b = lax.optimization_barrier((opened, taps_b))
    share_b = shares(taps_b, "y", 0)
    opened_b = ring_open(share_b, "y")
    part_a1 = ring_close(share_a, "x", *opened).reshape(4, 3 * block, channels)
    part_b1 = ring_close(share_b, "y", *opened_b).reshape(4, 3 * block, channels)
    part_a = direct_scatter(lambda places: ahead_of(part_a1, "y", places), "y")
    part_b = direct_scatter(lambda places: ahead_of(part_b1, "x", places), "x")
    part = jnp.concatenate([part_a, part_b], 0)
    part = lax.all_to_all(part.reshape(8, -1, channels), "z", 0, 0)
    part = jnp.sum(part.astype(F32), axis=0).astype(BF16)
    part = lax.all_to_all(jnp.broadcast_to(part[None], (8,) + part.shape), "z", 0, 0)
    mine = part.reshape(6, block, channels)
    other = lax.ppermute(mine, "core", both)
    total = jnp.concatenate(
        [jnp.where(first_core, mine, other), jnp.where(first_core, other, mine)], 0
    ).astype(F32)
    squares = jnp.sum(jnp.square(total)).reshape(1, 1, 1) + jnp.zeros((frames, 1, 128), F32)
    squares = lax.all_to_all(squares, ("y", "x"), 0, 0)
    squares = jnp.sum(squares[:, 0, 0])
    factor = clip_factor(squares, channels)
    row_start = frame * block
    spatial_here = lax.dynamic_slice(spatial_weight, (0, row_start, 0), (9, block, channels))
    temporal_here = lax.dynamic_slice(temporal_weight, (0, row_start, 0), (3, block, channels))
    new_spatial = spatial_here.astype(F32) - factor * total[:9]
    new_temporal = temporal_here.astype(F32) - factor * total[9:]
    return (new_spatial, new_temporal)


def solution(mesh):
    names = tuple(SIZES)
    grid = Mesh(mesh.devices.reshape(tuple(SIZES.values())), names)
    rows, frame = ("z", "core"), ("y", "x")
    in_specs = (P(rows, frame, None, None), P(rows, frame, None, None), P(rows), P(), P())
    out_specs = (P(None, frame, None), P(None, frame, None))
    return jax.shard_map(
        on_device, mesh=grid, in_specs=in_specs, out_specs=out_specs, check_vma=False
    )
```

```python
import math

import jax
import jax.numpy as jnp
from jax import lax
from jax.experimental import pallas as pl
from jax.experimental.pallas import tpu as pltpu
from jax.sharding import Mesh
from jax.sharding import PartitionSpec as P


WIDTH = 64
F32 = jnp.float32
BF16 = jnp.bfloat16
SIZES = {"z": 8, "core": 2, "y": 4, "x": 4}


def embed(timesteps, channels):
    half_width = channels // 2
    frequencies = jnp.exp(
        -math.log(10000.0) * jnp.arange(half_width, dtype=jnp.float32) / half_width
    )
    angles = timesteps.astype(jnp.float32)[:, None] * frequencies[None, :]
    return jnp.concatenate([jnp.sin(angles), jnp.cos(angles)], axis=1)


def clip_factor(squares, channels):
    max_norm = 0.5 * math.sqrt(12.0) * channels
    return jnp.minimum(1.0, max_norm / (jnp.sqrt(squares) + 1e-06))


def hop(value, axis, step):
    size = SIZES[axis]
    return lax.ppermute(value, axis, [(i, (i + step) % size) for i in range(size)])


def add(left, right):
    return (left.astype(F32) + right.astype(F32)).astype(BF16)


def both_ways(up, down, axis):
    up = hop(up, axis, 1)
    down = hop(down, axis, 3)
    return up, down


def ring_open(share, axis):
    far = share(2)
    half = far.shape[0] // 2
    return both_ways(far[:half], far[half:], axis)


def ring_close(share, axis, from_left, from_right):
    half = from_left.shape[0]
    ahead = share(1)
    behind = share(3)
    ahead = jnp.concatenate([add(ahead[:half], from_left), ahead[half:]], 0)
    behind = jnp.concatenate([behind[:half], add(behind[half:], from_right)], 0)
    from_left, from_right = both_ways(ahead, behind, axis)
    return (share(0).astype(F32) + from_left.astype(F32) + from_right.astype(F32)).astype(BF16)


def direct_scatter(share, axis):
    far = hop(share(2), axis, 2)
    left = hop(share(1), axis, 1)
    right = hop(share(3), axis, 3)
    total = share(0).astype(F32) + left.astype(F32) + right.astype(F32) + far.astype(F32)
    return total.astype(BF16)


def shift_rows(value, by):
    rows = value.shape[1]
    if by == 0:
        return value
    if by > 0:
        return jnp.pad(value[:, by:], ((0, 0), (0, by), (0, 0)))
    return jnp.pad(value[:, : rows + by], ((0, 0), (-by, 0), (0, 0)))


def shift_cols(value, by):
    if by == 0:
        return value
    q = lax.broadcasted_iota(jnp.int32, (1, value.shape[1], 1), 1) % WIDTH
    edge = q == (WIDTH - 1 if by > 0 else 0)
    return jnp.where(edge, jnp.zeros((), value.dtype), shift_rows(value, by))


def rows_dot(left, right):
    return lax.dot_general(left, right, (((0,), (0,)), ((), ())), preferred_element_type=F32)


def store_shares(axis, place, step, acc, shares):
    block = acc.shape[0] // 16
    for j, share in enumerate(shares):
        owner = lax.rem(place + j, 4)
        for k in range(4):
            start = (k * 4 + owner) * block if axis == "x" else (owner * 4 + k) * block
            rows = acc[pl.ds(pl.multiple_of(start, 8), block), :]
            share[k, step] = rows.astype(BF16)


def edge_kernel(where, turned, turned_far, grad, grad_far, *refs):
    *shares, acc = refs
    step = pl.program_id(0)
    inner = grad.shape[0] - WIDTH
    top = pl.multiple_of((1 + where[0]) * WIDTH, WIDTH)
    below = pl.multiple_of((1 - where[0]) * WIDTH, WIDTH)
    acc[...] = rows_dot(turned[0, pl.ds(top, inner), :], grad[pl.ds(below, inner), :])
    acc[...] += rows_dot(turned_far[0, pl.ds(top, inner), :], grad_far[pl.ds(below, inner), :])
    store_shares("x", where[1], step, acc, shares)


def mixed_kernel(where, turned, turned_far, grad, grad_far, cots, gate, cots_far, gate_far, *refs):
    *shares, acc = refs
    step = pl.program_id(0)
    pixels = grad.shape[0]

    @pl.when(where[0] == 0)
    def _():
        acc[...] = rows_dot(turned[0, WIDTH : WIDTH + pixels, :], grad[...])
        acc[...] += rows_dot(turned_far[0, WIDTH : WIDTH + pixels, :], grad_far[...])

    @pl.when(where[0] == 1)
    def _():
        acc[...] = rows_dot(gate[0], cots[0])
        acc[...] += rows_dot(gate_far[0], cots_far[0])

    store_shares("y", where[1], step, acc, shares)


def taps(kernel, where, arrays, blocks):
    channels = arrays[0].shape[-1]
    block = channels // 16

    def spec(array, lead):
        if lead is None:
            return pl.BlockSpec(array.shape, lambda e, where: (0,) * array.ndim)
        return pl.BlockSpec((1,) + array.shape[1:], lambda e, where: (lead(e), 0, 0))

    share = jax.ShapeDtypeStruct((4, 3, block, channels), BF16)
    out = pl.pallas_call(
        kernel,
        out_shape=[share] * 4,
        grid_spec=pltpu.PrefetchScalarGridSpec(
            num_scalar_prefetch=1,
            grid=(3,),
            in_specs=[spec(a, b) for a, b in zip(arrays, blocks)],
            out_specs=[pl.BlockSpec(share.shape, lambda e, where: (0, 0, 0, 0))] * 4,
            scratch_shapes=[pltpu.VMEM((channels, channels), F32)],
        ),
        compiler_params=pltpu.CompilerParams(vmem_limit_bytes=20 << 20),
        cost_estimate=pl.CostEstimate(
            flops=6 * 1024 * channels * channels, bytes_accessed=12 << 20, transcendentals=0
        ),
    )(where, *arrays)
    return [o.reshape(12 * block, channels) for o in out]


def back_kernel(where, before, here, after, weight, slope, gated, grad, lend, acc):
    def product(value, k):
        return lax.dot_general(
            value, weight[k], (((1,), (1,)), ((), ())), preferred_element_type=F32
        )

    lend[1] = here[...]
    lend[3] = gated[...]
    none = jnp.zeros(here.shape, here.dtype)
    acc[...] = product(here[...], 1)

    @pl.when(where[0] == 15)
    def _():
        lend[0] = none

    @pl.when(where[0] < 15)
    def _():
        lend[0] = after[...]
        acc[...] += product(after[...], 0)

    @pl.when(where[0] == 0)
    def _():
        lend[2] = none

    @pl.when(where[0] > 0)
    def _():
        lend[2] = before[...]
        acc[...] += product(before[...], 2)

    grad[...] = (acc[...].astype(BF16).astype(F32) * slope[...]).astype(BF16)


def back(where, before, here, after, weight, slope, gated):
    pixels, channels = here.shape

    def whole(array):
        return pl.BlockSpec(array.shape, lambda t, where: (0,) * array.ndim)

    arrays = (before, here, after, weight, slope, gated)
    outs = [
        jax.ShapeDtypeStruct((pixels, channels), BF16),
        jax.ShapeDtypeStruct((4, pixels, channels), BF16),
    ]
    return pl.pallas_call(
        back_kernel,
        out_shape=outs,
        grid_spec=pltpu.PrefetchScalarGridSpec(
            num_scalar_prefetch=1,
            grid=(1,),
            in_specs=[whole(a) for a in arrays],
            out_specs=[whole(o) for o in outs],
            scratch_shapes=[pltpu.VMEM((pixels, channels), F32)],
        ),
        compiler_params=pltpu.CompilerParams(vmem_limit_bytes=20 << 20),
        cost_estimate=pl.CostEstimate(
            flops=6 * pixels * channels * channels, bytes_accessed=8 << 20, transcendentals=0
        ),
        name="back",
    )(where, *arrays)


def forward_kernel(turned, weight, gated, slope, acc):
    tap = pl.program_id(0)
    pixels = acc.shape[0]
    start = pl.multiple_of(tap // 3 * WIDTH, WIDTH)
    here = turned[tap % 3, pl.ds(start, pixels), :]
    term = jnp.dot(here, weight[0], preferred_element_type=F32)

    @pl.when(tap == 0)
    def _():
        acc[...] = term

    @pl.when(tap > 0)
    def _():
        acc[...] += term

    @pl.when(tap == 8)
    def _():
        pre_act = acc[...]
        logistic = jax.nn.sigmoid(pre_act)
        gated[...] = (pre_act * logistic).astype(BF16)
        slope[...] = logistic * (1.0 + pre_act * (1.0 - logistic))


def forward(turned, weight):
    pixels = turned.shape[1] - 2 * WIDTH
    channels = turned.shape[2]
    whole = pl.BlockSpec((pixels, channels), lambda t: (0, 0))
    return pl.pallas_call(
        forward_kernel,
        out_shape=[
            jax.ShapeDtypeStruct((pixels, channels), BF16),
            jax.ShapeDtypeStruct((pixels, channels), F32),
        ],
        grid=(9,),
        in_specs=[
            pl.BlockSpec(turned.shape, lambda t: (0, 0, 0)),
            pl.BlockSpec((1, channels, channels), lambda t: (t, 0, 0)),
        ],
        out_specs=[whole, whole],
        scratch_shapes=[pltpu.VMEM((pixels, channels), F32)],
        compiler_params=pltpu.CompilerParams(vmem_limit_bytes=20 << 20),
        cost_estimate=pl.CostEstimate(
            flops=18 * pixels * channels * channels,
            bytes_accessed=12 << 20,
            transcendentals=pixels * channels,
        ),
        name="forward",
    )(turned, weight)


def on_device(latents, cotangent, timesteps, spatial_weight, temporal_weight):
    channels = latents.shape[3]
    pixels = latents.shape[2]
    frames = SIZES["y"] * SIZES["x"]
    block = channels // frames
    cot = cotangent.reshape(pixels, channels)
    core, y_here, x_here = (lax.axis_index(name) for name in ("core", "y", "x"))
    frame = y_here * SIZES["x"] + x_here
    places = dict(
        frame=frame.reshape(1).astype(jnp.int32),
        edge=jnp.stack([core, x_here]).astype(jnp.int32),
        mixed=jnp.stack([core, y_here]).astype(jnp.int32),
        y=[(y_here + j) & 3 for j in range(4)],
        x=[(x_here + j) & 3 for j in range(4)],
        first=jnp.broadcast_to(core == 0, (1, 1, 1)),
        row=frame * block,
    )
    places, cot, latents = lax.optimization_barrier((places, cot, latents))
    cot_prev = lax.ppermute(cot, ("y", "x"), [(f, (f + 1) % frames) for f in range(frames)])
    cot_next = lax.ppermute(cot, ("y", "x"), [((f + 1) % frames, f) for f in range(frames)])

    both = [(0, 1), (1, 0)]
    shifts = embed(timesteps, channels)
    activated = jax.nn.silu(latents.reshape(pixels, channels).astype(F32) + shifts).astype(BF16)

    border = ((0, 0), (WIDTH, WIDTH), (0, 0))
    turned = jnp.concatenate(
        [jnp.pad(shift_cols(activated[None], e - 1), border) for e in range(3)], 0
    )
    turned_far = lax.ppermute(turned, "core", both)
    gated, slope = forward(turned, spatial_weight)
    grad, lend = back(places["frame"], cot_prev, cot, cot_next, temporal_weight, slope, gated)
    grad_far = lax.ppermute(grad, "core", both)
    grad_far, lend = lax.optimization_barrier((grad_far, lend))
    lent = lax.ppermute(lend, "core", both)

    step_of = lambda e: e
    sources = (turned, turned_far, grad, grad_far)
    shares_a = taps(edge_kernel, places["edge"], sources, (step_of, step_of, None, None))
    share_a = shares_a.__getitem__
    opened = ring_open(share_a, "x")
    gate_of = lambda e: 3
    shares_b = taps(
        mixed_kernel,
        places["mixed"],
        sources + (lend, lend, lent, lent),
        (step_of, step_of, None, None, step_of, gate_of, step_of, gate_of),
    )
    opened, shares_b = lax.optimization_barrier((opened, shares_b))
    share_b = shares_b.__getitem__
    opened_b = ring_open(share_b, "y")
    part_a1 = ring_close(share_a, "x", *opened).reshape(4, 3 * block, channels)
    part_b1 = ring_close(share_b, "y", *opened_b).reshape(4, 3 * block, channels)

    def pick(value, axis):
        return lambda j: lax.dynamic_index_in_dim(value, places[axis][j], 0, keepdims=False, allow_negative_indices=False)

    part_a = direct_scatter(pick(part_a1, "y"), "y")
    part_b = direct_scatter(pick(part_b1, "x"), "x")
    part = jnp.concatenate([part_a, part_b], 0)
    part = lax.all_to_all(part.reshape(8, -1, channels), "z", 0, 0)
    part = jnp.sum(part.astype(F32), axis=0).astype(BF16)
    part = lax.all_to_all(jnp.broadcast_to(part[None], (8,) + part.shape), "z", 0, 0)
    mine = part.reshape(6, block, channels)
    other = lax.ppermute(mine, "core", both)
    total = jnp.concatenate(
        [jnp.where(places["first"], mine, other), jnp.where(places["first"], other, mine)], 0
    ).astype(F32)
    squares = jnp.sum(jnp.square(total)).reshape(1, 1, 1) + jnp.zeros((frames, 1, 128), F32)
    squares = lax.all_to_all(squares, ("y", "x"), 0, 0)
    squares = jnp.sum(squares[:, 0, 0])
    factor = clip_factor(squares, channels)
    row_start = places["row"]
    spatial_here = lax.dynamic_slice(spatial_weight, (0, row_start, 0), (9, block, channels), allow_negative_indices=False)
    temporal_here = lax.dynamic_slice(temporal_weight, (0, row_start, 0), (3, block, channels), allow_negative_indices=False)
    new_spatial = spatial_here.astype(F32) - factor * total[:9]
    new_temporal = temporal_here.astype(F32) - factor * total[9:]
    return (new_spatial, new_temporal)


def solution(mesh):
    names = tuple(SIZES)
    grid = Mesh(mesh.devices.reshape(tuple(SIZES.values())), names)
    rows, frame = ("z", "core"), ("y", "x")
    in_specs = (P(rows, frame, None, None), P(rows, frame, None, None), P(rows), P(), P())
    out_specs = (P(None, frame, None), P(None, frame, None))

    return jax.shard_map(
        on_device, mesh=grid, in_specs=in_specs, out_specs=out_specs, check_vma=False
    )
```

```python
import math

import jax
import jax.numpy as jnp
from jax import lax
from jax.experimental import pallas as pl
from jax.experimental.pallas import tpu as pltpu
from jax.sharding import Mesh
from jax.sharding import PartitionSpec as P


WIDTH = 64
F32 = jnp.float32
BF16 = jnp.bfloat16
SIZES = {"z": 8, "core": 2, "y": 4, "x": 4}


def embed(timesteps, channels):
    half_width = channels // 2
    frequencies = jnp.exp(
        -math.log(10000.0) * jnp.arange(half_width, dtype=jnp.float32) / half_width
    )
    angles = timesteps.astype(jnp.float32)[:, None] * frequencies[None, :]
    return jnp.concatenate([jnp.sin(angles), jnp.cos(angles)], axis=1)


def clip_factor(squares, channels):
    max_norm = 0.5 * math.sqrt(12.0) * channels
    return jnp.minimum(1.0, max_norm / (jnp.sqrt(squares) + 1e-06))


def hop(value, axis, step):
    size = SIZES[axis]
    return lax.ppermute(value, axis, [(i, (i + step) % size) for i in range(size)])


def add(left, right):
    return (left.astype(F32) + right.astype(F32)).astype(BF16)


def both_ways(up, down, axis):
    up = hop(up, axis, 1)
    down = hop(down, axis, 3)
    return up, down


def ring_open(share, axis):
    far = share(2)
    half = far.shape[0] // 2
    return both_ways(far[:half], far[half:], axis)


def ring_close(share, axis, from_left, from_right):
    half = from_left.shape[0]
    ahead = share(1)
    behind = share(3)
    ahead = jnp.concatenate([add(ahead[:half], from_left), ahead[half:]], 0)
    behind = jnp.concatenate([behind[:half], add(behind[half:], from_right)], 0)
    from_left, from_right = both_ways(ahead, behind, axis)
    return (share(0).astype(F32) + from_left.astype(F32) + from_right.astype(F32)).astype(BF16)


def direct_scatter(share, axis):
    far = hop(share(2), axis, 2)
    left = hop(share(1), axis, 1)
    right = hop(share(3), axis, 3)
    total = share(0).astype(F32) + left.astype(F32) + right.astype(F32) + far.astype(F32)
    return total.astype(BF16)


def shift_rows(value, by):
    rows = value.shape[1]
    if by == 0:
        return value
    if by > 0:
        return jnp.pad(value[:, by:], ((0, 0), (0, by), (0, 0)))
    return jnp.pad(value[:, : rows + by], ((0, 0), (-by, 0), (0, 0)))


def shift_cols(value, by):
    if by == 0:
        return value
    q = lax.broadcasted_iota(jnp.int32, (1, value.shape[1], 1), 1) % WIDTH
    edge = q == (WIDTH - 1 if by > 0 else 0)
    return jnp.where(edge, jnp.zeros((), value.dtype), shift_rows(value, by))


def rows_dot(left, right):
    return lax.dot_general(left, right, (((0,), (0,)), ((), ())), preferred_element_type=F32)


def store_shares(axis, place, step, acc, shares):
    block = acc.shape[0] // 16
    for j, share in enumerate(shares):
        owner = lax.rem(place + j, 4)
        for k in range(4):
            start = (k * 4 + owner) * block if axis == "x" else (owner * 4 + k) * block
            rows = acc[pl.ds(pl.multiple_of(start, 8), block), :]
            share[k, step] = rows.astype(BF16)


def edge_kernel(where, turned, turned_far, grad, grad_far, *refs):
    *shares, acc = refs
    step = pl.program_id(0)
    inner = grad.shape[0] - WIDTH
    top = pl.multiple_of((1 + where[0]) * WIDTH, WIDTH)
    below = pl.multiple_of((1 - where[0]) * WIDTH, WIDTH)
    acc[...] = rows_dot(turned[0, pl.ds(top, inner), :], grad[pl.ds(below, inner), :])
    acc[...] += rows_dot(turned_far[0, pl.ds(top, inner), :], grad_far[pl.ds(below, inner), :])
    store_shares("x", where[1], step, acc, shares)


def mixed_kernel(where, turned, turned_far, grad, grad_far, cots, gate, cots_far, gate_far, *refs):
    *shares, acc = refs
    step = pl.program_id(0)
    pixels = grad.shape[0]

    @pl.when(where[0] == 0)
    def _():
        acc[...] = rows_dot(turned[0, WIDTH : WIDTH + pixels, :], grad[...])
        acc[...] += rows_dot(turned_far[0, WIDTH : WIDTH + pixels, :], grad_far[...])

    @pl.when(where[0] == 1)
    def _():
        acc[...] = rows_dot(gate[0], cots[0])
        acc[...] += rows_dot(gate_far[0], cots_far[0])

    store_shares("y", where[1], step, acc, shares)


def taps(kernel, where, arrays, blocks):
    channels = arrays[0].shape[-1]
    block = channels // 16

    def spec(array, lead):
        if lead is None:
            return pl.BlockSpec(array.shape, lambda e, where: (0,) * array.ndim)
        return pl.BlockSpec((1,) + array.shape[1:], lambda e, where: (lead(e), 0, 0))

    share = jax.ShapeDtypeStruct((4, 3, block, channels), BF16)
    out = pl.pallas_call(
        kernel,
        out_shape=[share] * 4,
        grid_spec=pltpu.PrefetchScalarGridSpec(
            num_scalar_prefetch=1,
            grid=(3,),
            in_specs=[spec(a, b) for a, b in zip(arrays, blocks)],
            out_specs=[pl.BlockSpec(share.shape, lambda e, where: (0, 0, 0, 0))] * 4,
            scratch_shapes=[pltpu.VMEM((channels, channels), F32)],
        ),
        compiler_params=pltpu.CompilerParams(vmem_limit_bytes=20 << 20),
        cost_estimate=pl.CostEstimate(
            flops=6 * 1024 * channels * channels, bytes_accessed=12 << 20, transcendentals=0
        ),
    )(where, *arrays)
    return [o.reshape(12 * block, channels) for o in out]


def back_kernel(where, before, here, after, weight, slope, gated, grad, lend, acc):
    def product(value, k):
        return lax.dot_general(
            value, weight[k], (((1,), (1,)), ((), ())), preferred_element_type=F32
        )

    lend[1] = here[...]
    lend[3] = gated[...]
    none = jnp.zeros(here.shape, here.dtype)
    acc[...] = product(here[...], 1)

    @pl.when(where[0] == 15)
    def _():
        lend[0] = none

    @pl.when(where[0] < 15)
    def _():
        lend[0] = after[...]
        acc[...] += product(after[...], 0)

    @pl.when(where[0] == 0)
    def _():
        lend[2] = none

    @pl.when(where[0] > 0)
    def _():
        lend[2] = before[...]
        acc[...] += product(before[...], 2)

    grad[...] = (acc[...].astype(BF16).astype(F32) * slope[...]).astype(BF16)


def back(where, before, here, after, weight, slope, gated):
    pixels, channels = here.shape

    def whole(array):
        return pl.BlockSpec(array.shape, lambda t, where: (0,) * array.ndim)

    arrays = (before, here, after, weight, slope, gated)
    outs = [
        jax.ShapeDtypeStruct((pixels, channels), BF16),
        jax.ShapeDtypeStruct((4, pixels, channels), BF16),
    ]
    return pl.pallas_call(
        back_kernel,
        out_shape=outs,
        grid_spec=pltpu.PrefetchScalarGridSpec(
            num_scalar_prefetch=1,
            grid=(1,),
            in_specs=[whole(a) for a in arrays],
            out_specs=[whole(o) for o in outs],
            scratch_shapes=[pltpu.VMEM((pixels, channels), F32)],
        ),
        compiler_params=pltpu.CompilerParams(vmem_limit_bytes=20 << 20),
        cost_estimate=pl.CostEstimate(
            flops=6 * pixels * channels * channels, bytes_accessed=8 << 20, transcendentals=0
        ),
        name="back",
    )(where, *arrays)


def forward_kernel(turned, weight, gated, slope, acc):
    tap = pl.program_id(0)
    pixels = acc.shape[0]
    start = pl.multiple_of(tap // 3 * WIDTH, WIDTH)
    here = turned[tap % 3, pl.ds(start, pixels), :]
    term = jnp.dot(here, weight[0], preferred_element_type=F32)

    @pl.when(tap == 0)
    def _():
        acc[...] = term

    @pl.when(tap > 0)
    def _():
        acc[...] += term

    @pl.when(tap == 8)
    def _():
        pre_act = acc[...]
        logistic = jax.nn.sigmoid(pre_act)
        gated[...] = (pre_act * logistic).astype(BF16)
        slope[...] = logistic * (1.0 + pre_act * (1.0 - logistic))


def forward(turned, weight):
    pixels = turned.shape[1] - 2 * WIDTH
    channels = turned.shape[2]
    whole = pl.BlockSpec((pixels, channels), lambda t: (0, 0))
    return pl.pallas_call(
        forward_kernel,
        out_shape=[
            jax.ShapeDtypeStruct((pixels, channels), BF16),
            jax.ShapeDtypeStruct((pixels, channels), F32),
        ],
        grid=(9,),
        in_specs=[
            pl.BlockSpec(turned.shape, lambda t: (0, 0, 0)),
            pl.BlockSpec((1, channels, channels), lambda t: (t, 0, 0)),
        ],
        out_specs=[whole, whole],
        scratch_shapes=[pltpu.VMEM((pixels, channels), F32)],
        compiler_params=pltpu.CompilerParams(vmem_limit_bytes=20 << 20),
        cost_estimate=pl.CostEstimate(
            flops=18 * pixels * channels * channels,
            bytes_accessed=12 << 20,
            transcendentals=pixels * channels,
        ),
        name="forward",
    )(turned, weight)


def squares_kernel(mine, other, out):
    total = jnp.zeros(mine.shape[1:], F32)
    for tap in range(mine.shape[0]):
        total = total + jnp.square(mine[tap].astype(F32)) + jnp.square(other[tap].astype(F32))
    total = jnp.sum(jnp.sum(total, axis=0, keepdims=True), axis=1, keepdims=True)
    out[...] = jnp.broadcast_to(total.reshape(1, 1, 1), out.shape)


def step_kernel(where, squares, mine, other, spatial, temporal, new_spatial, new_temporal):
    channels = spatial.shape[2]
    total = jnp.sum(squares[:, 0, :], axis=0, keepdims=True)[:, :1]
    factor = clip_factor(total, channels)
    first = where[0] == 0
    for tap in range(12):
        half = tap % 6
        near, far = (mine, other) if tap < 6 else (other, mine)
        part = jnp.where(first, near[half].astype(F32), far[half].astype(F32))
        if tap < 9:
            new_spatial[tap] = spatial[tap].astype(F32) - factor * part
        else:
            new_temporal[tap - 9] = temporal[tap - 9].astype(F32) - factor * part


def clipped_step(where, squares, mine, other, spatial, temporal):
    def whole(array):
        return pl.BlockSpec(array.shape, lambda t, where: (0,) * array.ndim)

    arrays = (squares, mine, other, spatial, temporal)
    outs = [jax.ShapeDtypeStruct(a.shape, F32) for a in (spatial, temporal)]
    return pl.pallas_call(
        step_kernel,
        out_shape=outs,
        grid_spec=pltpu.PrefetchScalarGridSpec(
            num_scalar_prefetch=1,
            grid=(1,),
            in_specs=[whole(a) for a in arrays],
            out_specs=[whole(o) for o in outs],
        ),
        compiler_params=pltpu.CompilerParams(vmem_limit_bytes=20 << 20),
        name="step",
    )(where, *arrays)


def on_device(latents, cotangent, timesteps, spatial_weight, temporal_weight):
    channels = latents.shape[3]
    pixels = latents.shape[2]
    frames = SIZES["y"] * SIZES["x"]
    block = channels // frames
    cot = cotangent.reshape(pixels, channels)
    core, y_here, x_here = (lax.axis_index(name) for name in ("core", "y", "x"))
    frame = y_here * SIZES["x"] + x_here
    places = dict(
        frame=frame.reshape(1).astype(jnp.int32),
        edge=jnp.stack([core, x_here]).astype(jnp.int32),
        mixed=jnp.stack([core, y_here]).astype(jnp.int32),
        y=[(y_here + j) & 3 for j in range(4)],
        x=[(x_here + j) & 3 for j in range(4)],
        row=frame * block,
    )
    places, cot, latents = lax.optimization_barrier((places, cot, latents))
    cot_prev = lax.ppermute(cot, ("y", "x"), [(f, (f + 1) % frames) for f in range(frames)])
    cot_next = lax.ppermute(cot, ("y", "x"), [((f + 1) % frames, f) for f in range(frames)])

    both = [(0, 1), (1, 0)]
    shifts = embed(timesteps, channels)
    activated = jax.nn.silu(latents.reshape(pixels, channels).astype(F32) + shifts).astype(BF16)

    border = ((0, 0), (WIDTH, WIDTH), (0, 0))
    turned = jnp.concatenate(
        [jnp.pad(shift_cols(activated[None], e - 1), border) for e in range(3)], 0
    )
    turned_far = lax.ppermute(turned, "core", both)
    gated, slope = forward(turned, spatial_weight)
    grad, lend = back(places["frame"], cot_prev, cot, cot_next, temporal_weight, slope, gated)
    grad_far = lax.ppermute(grad, "core", both)
    grad_far, lend = lax.optimization_barrier((grad_far, lend))
    lent = lax.ppermute(lend, "core", both)

    step_of = lambda e: e
    sources = (turned, turned_far, grad, grad_far)
    shares_a = taps(edge_kernel, places["edge"], sources, (step_of, step_of, None, None))
    share_a = shares_a.__getitem__
    opened = ring_open(share_a, "x")
    gate_of = lambda e: 3
    shares_b = taps(
        mixed_kernel,
        places["mixed"],
        sources + (lend, lend, lent, lent),
        (step_of, step_of, None, None, step_of, gate_of, step_of, gate_of),
    )
    share_b = shares_b.__getitem__
    opened_b = ring_open(share_b, "y")
    row_start = places["row"]
    spatial_here = lax.dynamic_slice(
        spatial_weight, (0, row_start, 0), (9, block, channels), allow_negative_indices=False
    )
    temporal_here = lax.dynamic_slice(
        temporal_weight, (0, row_start, 0), (3, block, channels), allow_negative_indices=False
    )
    opened_b, spatial_here, temporal_here = lax.optimization_barrier(
        (opened_b, spatial_here, temporal_here)
    )
    part_a1 = ring_close(share_a, "x", *opened).reshape(4, 3 * block, channels)
    part_b1 = ring_close(share_b, "y", *opened_b).reshape(4, 3 * block, channels)

    def pick(value, axis):
        return lambda j: lax.dynamic_index_in_dim(value, places[axis][j], 0, keepdims=False, allow_negative_indices=False)

    part_a = direct_scatter(pick(part_a1, "y"), "y")
    part_b = direct_scatter(pick(part_b1, "x"), "x")
    part = jnp.concatenate([part_a, part_b], 0)
    part = lax.all_to_all(part.reshape(8, -1, channels), "z", 0, 0)
    part = jnp.sum(part.astype(F32), axis=0).astype(BF16)
    part = lax.all_to_all(jnp.broadcast_to(part[None], (8,) + part.shape), "z", 0, 0)
    mine = part.reshape(6, block, channels)
    other = lax.ppermute(mine, "core", both)
    squares = pl.pallas_call(
        squares_kernel,
        out_shape=jax.ShapeDtypeStruct((frames, 1, 128), F32),
        compiler_params=pltpu.CompilerParams(vmem_limit_bytes=20 << 20),
        name="squares",
    )(mine, other)
    squares = lax.all_to_all(squares, ("y", "x"), 0, 0)
    return clipped_step(places["edge"], squares, mine, other, spatial_here, temporal_here)


def solution(mesh):
    names = tuple(SIZES)
    grid = Mesh(mesh.devices.reshape(tuple(SIZES.values())), names)
    rows, frame = ("z", "core"), ("y", "x")
    in_specs = (P(rows, frame, None, None), P(rows, frame, None, None), P(rows), P(), P())
    out_specs = (P(None, frame, None), P(None, frame, None))

    return jax.shard_map(
        on_device, mesh=grid, in_specs=in_specs, out_specs=out_specs, check_vma=False
    )
```
